512 devices in a mesh: mem: 4 (over x), col: 128 (over z, y, core).
Axes of the slice: x: 4, y: 4, z: 16, core: 2. Of those that a mesh axis runs over, the one named last changes fastest.
Arguments:
- adj_final: float32 [16, 137, 65536], P('mem', None, 'col'), parts along dimension 0, may hold values from -60 to 60
- inverses: float32 [8, 512, 137, 137], P('mem', 'col'), parts along dimension 0, may hold values from 0 to 1
- dep_lists: int32 [8, 512, 5], P('mem', 'col'), parts along dimension 0, may hold values from 0 to 511, as said below
- dep_points: int32 [8, 4, 65536], P('mem', None, 'col'), parts along dimension 0, may hold values from 0 to 639, as said below
- weights: float32 [8, 4, 65536], P('mem', None, 'col'), parts along dimension 0, may hold values from 0 to 1, as said below
Outputs:
- adj_mid: float32 [16, 137, 65536], P('mem', None, 'col'), parts along dimension 0
- lanczos: float32 [16, 137, 65536], P('mem', None, 'col'), parts along dimension 0
The draws below stay inside these ranges and needn't reach their ends.
There are 4 independent parts, one for each index of `mem`. The reference program is written for one: setup_inputs(seed, part) draws one part's arguments, and reference() takes and returns one part's arrays. A program takes and returns all parts, laid end to end along the dimension named above; each array names one. Nothing has to cross between parts.
Inputs may be any that keep to these rules, and one draw needn't show every extreme that they name: `dep_lists`: every entry of a block's list is a block within 2 blocks of that block, counting cyclically over all 512 blocks; the list's first entries are distinct and the rest repeat the block itself. `dep_points`: the slot of every point indexes one of the first entries of its arrival block's list. The 4 weights of a column are bilinear weights and sum to one.
All inputs are finite; a program needn't handle non-finite values.
Results may differ from the reference program's by a relative error of at most 0.0003.
Values sent between devices are 32-bit elements; how exact they have to be, the bound alone decides.
A program may use at most 64 MiB of HBM per device.

```python
import math
import jax
import jax.numpy as jnp
from jax import lax

LEVELS = 137
VARS = 4
BCOLS = 128
REACH = 2
SLOTS = 5
POINTS = 4
STEPS = 2
NBLK = 512
COLS = 65536


def slot_counts(key):
    key_counts = jax.random.fold_in(key, 17)
    key_start, key_strong, key_drawn = jax.random.split(key_counts, 3)
    blocks = jnp.arange(NBLK, dtype=jnp.int32)
    start = jax.random.randint(key_start, (STEPS, 1), 0, NBLK)
    band = (blocks[None, :] - start) % NBLK < max(NBLK // 4, 1)
    strong = jax.random.randint(key_strong, (STEPS, NBLK), 3, SLOTS + 1)
    drawn = jax.random.randint(key_drawn, (STEPS, NBLK), 1, 3)
    counts = jnp.where(band, strong, drawn).astype(jnp.int32)
    return counts.at[:, 0].set(SLOTS)


def draw_dep_lists(key, part):
    counts = slot_counts(key)
    key_lists = jax.random.fold_in(key, 29)
    width = 2 * REACH + 1
    scores = jax.random.randint(key_lists, (STEPS, NBLK, width), 0, 1 << 20) * width + jnp.arange(width, dtype=jnp.int32)
    order = jnp.argsort(scores, axis=-1).astype(jnp.int32)
    offsets = order[:, :, :SLOTS] - REACH
    used = jnp.arange(SLOTS, dtype=jnp.int32)[None, None, :] < counts[:, :, None]
    offsets = jnp.where(used, offsets, 0)
    blocks = jnp.arange(NBLK, dtype=jnp.int32)[None, :, None]
    return ((blocks + offsets) % NBLK).astype(jnp.int32)


def draw_dep_points(key, part):
    counts = slot_counts(key)
    key_points = jax.random.fold_in(key, 41)
    key_slot, key_within = jax.random.split(key_points, 2)
    per_column = jnp.repeat(counts, BCOLS, axis=1)
    raw = jax.random.randint(key_slot, (STEPS, POINTS, COLS), 0, 1 << 20)
    slot_ids = raw % per_column[:, None, :]
    within = jax.random.randint(key_within, (STEPS, POINTS, COLS), 0, BCOLS)
    points = (slot_ids * BCOLS + within).astype(jnp.int32)
    points = points.at[:, 0, 0].set((SLOTS - 1) * BCOLS + BCOLS - 1)
    points = points.at[:, 1, 0].set(0)
    return points


def draw_weights(key, part):
    key_east, key_north = jax.random.split(key, 2)
    east = jax.random.uniform(key_east, (STEPS, COLS), jnp.float32)
    north = jax.random.uniform(key_north, (STEPS, COLS), jnp.float32)
    stacked = jnp.stack([(1.0 - east) * (1.0 - north), east * (1.0 - north), (1.0 - east) * north, east * north], axis=1)
    return stacked.astype(jnp.float32)


def draw_adj_final(key, part):
    key_base, key_level = jax.random.split(key, 2)
    position = jnp.arange(COLS, dtype=jnp.float32) / COLS
    col_scale = jnp.exp(math.log(10.0) * (position - 0.5))[None, None, :]
    level_scale = jnp.exp(math.log(10.0) * (jax.random.uniform(key_level, (VARS, LEVELS, 1), jnp.float32) - 0.5))
    base = jnp.clip(jax.random.normal(key_base, (VARS, LEVELS, COLS), jnp.float32), -6.0, 6.0)
    return (base * col_scale * level_scale).astype(jnp.float32)


def draw_inverses(key, part):
    key_length, key_diag, key_spread = jax.random.split(key, 3)
    length = jnp.exp(jax.random.uniform(key_length, (STEPS, NBLK, 1, 1), jnp.float32, math.log(2.0), math.log(20.0)))
    level_rows = jnp.arange(LEVELS, dtype=jnp.float32)[:, None]
    level_cols = jnp.arange(LEVELS, dtype=jnp.float32)[None, :]
    distance = jnp.abs(level_rows - level_cols)
    diagonal = 1.0 + 0.3 * jax.random.uniform(key_diag, (STEPS, NBLK, LEVELS, 1), jnp.float32, -1.0, 1.0)
    spread = jax.random.uniform(key_spread, (STEPS, NBLK, LEVELS, LEVELS), jnp.float32, 0.0, 1.0)
    offdiag = 0.3 * jnp.exp(-distance / length) * spread
    matrix = jnp.where(distance == 0.0, diagonal, offdiag) / (1.0 + 0.3 * length)
    return matrix.astype(jnp.float32)


def setup_inputs(seed: int = 0, part: int = 0) -> dict:
    key_of = jax.random.split(jax.random.key(seed), 6)
    part_splits = jax.random.split(jax.random.fold_in(key_of[5], part), 6)
    adj_final = draw_adj_final(jax.random.fold_in(jax.random.fold_in(key_of[5], part), 71), part)
    inverses = draw_inverses(jax.random.fold_in(jax.random.fold_in(key_of[5], part), 71), part)
    dep_lists = draw_dep_lists(jax.random.fold_in(jax.random.fold_in(key_of[5], part), 71), part)
    dep_points = draw_dep_points(jax.random.fold_in(jax.random.fold_in(key_of[5], part), 71), part)
    weights = draw_weights(jax.random.fold_in(jax.random.fold_in(key_of[5], part), 71), part)
    return {"adj_final": adj_final, "inverses": inverses, "dep_lists": dep_lists, "dep_points": dep_points, "weights": weights}


eps_energy = 1e-06

def adjoint_step(adjoint, inverse, routes, points, weights):
    variables, levels, col_count = adjoint.shape
    block_count = col_count // BCOLS
    blocked = adjoint.reshape(variables, levels, block_count, BCOLS)
    diffused = jnp.einsum('blk,vlbc->vkbc', inverse, blocked, precision=lax.Precision.HIGHEST)
    columns_first = diffused.reshape(variables * levels, col_count).T
    slot_ids = points // BCOLS
    within = points % BCOLS
    arrival = jnp.arange(col_count, dtype=jnp.int32) // BCOLS
    target = (routes[arrival[None, :], slot_ids] * BCOLS + within).astype(jnp.int32)
    accumulated = jnp.zeros_like(columns_first)
    for point_index in range(POINTS):
        accumulated = accumulated.at[target[point_index]].add(weights[point_index][:, None] * columns_first)
    return accumulated.T.reshape(variables, levels, col_count)

def reference(adj_final, inverses, dep_lists, dep_points, weights):
    adjoint = adj_final
    adj_mid = adj_final
    for step_index in range(STEPS - 1, -1, -1):
        adjoint = adjoint_step(adjoint, inverses[step_index], dep_lists[step_index], dep_points[step_index], weights[step_index])
        if step_index == STEPS - 1:
            adj_mid = adjoint
    energy = jnp.mean(adjoint * adjoint)
    lanczos = adjoint / jnp.sqrt(energy + eps_energy)
    return (adj_mid, lanczos)
```

```python
import functools

import jax
import jax.numpy as jnp
from jax import lax
from jax.experimental import pallas as pl
from jax.experimental.pallas import tpu as pltpu
from jax.sharding import PartitionSpec as P

BCOLS = 128
REACH = 2
SLOTS = 5
POINTS = 4
STEPS = 2
PAIR = 2 * BCOLS
WINDOW = 3 * PAIR
EPS_ENERGY = 1e-06
GROUP = 8
CHUNKS = 2
MESH = pl.DeviceIdType.MESH
F32 = jnp.float32
BF16 = jnp.bfloat16


def halves(value):
    high = value.astype(BF16)
    low = (value - high.astype(F32)).astype(BF16)
    return high, low


def kernel(
    count,
    lists_hbm,
    points_hbm,
    weights_hbm,
    adj_hbm,
    inv_hbm,
    mid_ref,
    out_ref,
    lists_ref,
    points_ref,
    weights_ref,
    adj_in,
    inv_in,
    adj_pad,
    inv_pad,
    w_high,
    w_low,
    own,
    send_buf,
    recv_buf,
    near_buf,
    far_buf,
    small_sem,
    in_sem,
    inv_sem,
    send_sem,
    recv_sem,
    near_send,
    near_recv,
    far_send,
    far_recv,
):
    variables, padded, col_count = adj_pad.shape
    levels = inv_in.shape[-1]
    blocks = col_count // BCOLS
    pairs = blocks // 2
    tiles = pairs + 2
    per_chunk = variables // CHUNKS
    all_blocks = count * blocks
    me = lax.axis_index("col")
    up = lax.rem(me + 1, count)
    down = lax.rem(me + count - 1, count)
    group = min(GROUP, count)
    far_count = count // group
    near_me = lax.rem(me, group)
    far_me = me // group
    near_peers = [far_me * group + lax.rem(near_me + j, group) for j in range(1, group)]
    far_peers = [lax.rem(far_me + j, far_count) * group + near_me for j in range(1, far_count)]

    barrier = pltpu.get_barrier_semaphore()
    everyone = [up, down] + near_peers + far_peers
    for peer in everyone:
        pl.semaphore_signal(barrier, inc=1, device_id={"col": peer}, device_id_type=MESH)

    small_copies = [
        pltpu.make_async_copy(lists_hbm, lists_ref, small_sem.at[0]),
        pltpu.make_async_copy(points_hbm, points_ref, small_sem.at[1]),
        pltpu.make_async_copy(weights_hbm, weights_ref, small_sem.at[2]),
    ]
    inv_copies = {
        step: [
            pltpu.make_async_copy(
                inv_hbm.at[step, :, source, :], inv_in.at[step, source], inv_sem.at[step, source]
            )
            for source in range(blocks)
        ]
        for step in range(STEPS)
    }
    adj_copy = pltpu.make_async_copy(adj_hbm, adj_in, in_sem.at[0])
    for copy in small_copies + inv_copies[1] + [adj_copy] + inv_copies[0]:
        copy.start()

    whole = levels // 8 * 8
    stride = variables * blocks

    def pieces(v, source):
        first = source * variables + v
        yield slice(0, whole), pl.ds(first, whole, stride=stride)
        for level in range(whole, levels):
            yield slice(level, level + 1), pl.ds(level * stride + first, 1)

    def build(step):
        points = points_ref[step]
        slot_ids = points // BCOLS
        within = points % BCOLS
        for source in range(blocks):
            lanes = slice(source * BCOLS, (source + 1) * BCOLS)
            block = me * blocks + source
            slots = slot_ids[:, lanes]
            offset = jnp.zeros_like(slots)
            for slot in range(SLOTS):
                rel = lists_ref[step, source, slot] - block + REACH
                rel = jnp.where(rel < 0, rel + all_blocks, rel)
                rel = jnp.where(rel >= all_blocks, rel - all_blocks, rel)
                offset = jnp.where(slots == slot, rel, offset)
            column = offset * BCOLS + within[:, lanes]
            weight = weights_ref[step][:, lanes]
            parity = source % 2
            pair = source // 2
            half = slice(parity * BCOLS, (parity + 1) * BCOLS)
            empty = jnp.zeros((BCOLS, BCOLS), BF16)
            unused = slice(0, BCOLS) if parity else slice(SLOTS * BCOLS, WINDOW)
            w_high[step, pair, unused, half] = empty
            w_low[step, pair, unused, half] = empty
            for piece in range(SLOTS):
                rows = lax.broadcasted_iota(jnp.int32, (BCOLS, BCOLS), 0) + piece * BCOLS
                total = jnp.zeros((BCOLS, BCOLS), F32)
                for point in range(POINTS):
                    hit = rows == column[point : point + 1]
                    total = total + jnp.where(hit, weight[point : point + 1], 0.0)
                high, low = halves(total)
                place = slice((piece + parity) * BCOLS, (piece + parity + 1) * BCOLS)
                w_high[step, pair, place, half] = high
                w_low[step, pair, place, half] = low

    def pad_inverse(step):
        for source in range(blocks):
            inv_pad[source] = jnp.zeros((padded, padded), F32)
            inv_pad[source, 0:levels, 0:levels] = inv_in[step, source]

    def stacked_inverse(source):
        high, low = halves(inv_pad[source])
        return jnp.concatenate([high, low, high], axis=0)

    def diffuse(inverse, value):
        high, low = halves(value)
        return lax.dot_general(
            inverse,
            jnp.concatenate([high, high, low], axis=0),
            (((0,), (0,)), ((), ())),
            preferred_element_type=F32,
        )

    def diffused_pairs(block_value, inverses):
        result = []
        for pair in range(pairs):
            left = diffuse(inverses[2 * pair], block_value(2 * pair))
            right = diffuse(inverses[2 * pair + 1], block_value(2 * pair + 1))
            rows = [
                jnp.concatenate(
                    [left[:, v * BCOLS : (v + 1) * BCOLS], right[:, v * BCOLS : (v + 1) * BCOLS]], axis=1
                )
                for v in range(per_chunk)
            ]
            result.append(halves(jnp.concatenate(rows, axis=0)))
        return result

    def tile_sum(step, diffused, tile):
        left, right = [], []
        for pair in range(pairs):
            if 0 <= tile - pair <= 2:
                high, low = diffused[pair]
                place = slice((tile - pair) * PAIR, (tile - pair + 1) * PAIR)
                left += [high, low, high]
                matrix = w_high[step, pair, place, :]
                right += [matrix, matrix, w_low[step, pair, place, :]]
        return lax.dot_general(
            jnp.concatenate(left, axis=1),
            jnp.concatenate(right, axis=1),
            (((1,), (1,)), ((), ())),
            preferred_element_type=F32,
        )

    def halo_copy(exchange, chunk, way):
        return pltpu.make_async_remote_copy(
            src_ref=send_buf.at[exchange, chunk, way],
            dst_ref=recv_buf.at[exchange, chunk, way],
            send_sem=send_sem.at[exchange, chunk, way],
            recv_sem=recv_sem.at[exchange, chunk, way],
            device_id={"col": up if way else down},
            device_id_type=MESH,
        )

    def scatter(exchange, step, chunk, diffused, first):
        for way, tile in ((0, 0), (1, tiles - 1)):
            value = tile_sum(step, diffused, tile)
            for v in range(per_chunk):
                send_buf[exchange, chunk, way, v] = value[v * padded : (v + 1) * padded]
        if first:
            pl.semaphore_wait(barrier, len(everyone))
        for way in range(2):
            halo_copy(exchange, chunk, way).start()
        for tile in range(1, tiles - 1):
            value = tile_sum(step, diffused, tile)
            for v in range(per_chunk):
                own[chunk * per_chunk + v, :, (tile - 1) * PAIR : tile * PAIR] = value[
                    v * padded : (v + 1) * padded
                ]

    def arrived(exchange, chunk):
        for way in range(2):
            halo_copy(exchange, chunk, way).wait_recv()
        for v in range(per_chunk):
            row = chunk * per_chunk + v
            own[row, :, 0:PAIR] = own[row, :, 0:PAIR] + recv_buf[exchange, chunk, 1, v]
            last = slice(col_count - PAIR, col_count)
            own[row, :, last] = own[row, :, last] + recv_buf[exchange, chunk, 0, v]

    for copy in small_copies:
        copy.wait()
    build(1)
    for copy in inv_copies[1]:
        copy.wait()
    pad_inverse(1)
    inverses = [stacked_inverse(source) for source in range(blocks)]
    for v in range(variables):
        adj_pad[v, padded - 8 : padded, :] = jnp.zeros((8, col_count), F32)
    for chunk in range(CHUNKS):
        if chunk == 0:
            adj_copy.wait()
        for v in range(chunk * per_chunk, (chunk + 1) * per_chunk):
            for source in range(blocks):
                lanes = slice(source * BCOLS, (source + 1) * BCOLS)
                for part, rows in pieces(v, source):
                    adj_pad[v, part, lanes] = adj_in[rows, :]

        def block_value(source, chunk=chunk):
            lanes = slice(source * BCOLS, (source + 1) * BCOLS)
            return jnp.concatenate(
                [adj_pad[v, :, lanes] for v in range(chunk * per_chunk, (chunk + 1) * per_chunk)], axis=1
            )

        scatter(0, 1, chunk, diffused_pairs(block_value, inverses), chunk == 0)

    build(0)
    for copy in inv_copies[0]:
        copy.wait()
    pad_inverse(0)
    inverses = [stacked_inverse(source) for source in range(blocks)]
    for chunk in range(CHUNKS):
        arrived(0, chunk)
        for v in range(chunk * per_chunk, (chunk + 1) * per_chunk):
            for source in range(blocks):
                for part, rows in pieces(v, source):
                    mid_ref[rows, :] = own[v, part, source * BCOLS : (source + 1) * BCOLS]

        def block_value(source, chunk=chunk):
            lanes = slice(source * BCOLS, (source + 1) * BCOLS)
            return jnp.concatenate(
                [own[v, :, lanes] for v in range(chunk * per_chunk, (chunk + 1) * per_chunk)], axis=1
            )

        scatter(1, 0, chunk, diffused_pairs(block_value, inverses), False)

    total = jnp.zeros((8, BCOLS), F32)
    for chunk in range(CHUNKS):
        arrived(1, chunk)
        for v in range(chunk * per_chunk, (chunk + 1) * per_chunk):
            value = own[v]
            square = value * value
            by_lane = square[:, 0:BCOLS]
            for block in range(1, blocks):
                by_lane = by_lane + square[:, block * BCOLS : (block + 1) * BCOLS]
            total = total + jnp.sum(by_lane.reshape(padded // 8, 8, BCOLS), axis=0)

    near_buf[near_me] = total
    near_copies = [
        pltpu.make_async_remote_copy(
            src_ref=near_buf.at[near_me],
            dst_ref=near_buf.at[near_me],
            send_sem=near_send.at[j],
            recv_sem=near_recv.at[near_me],
            device_id={"col": peer},
            device_id_type=MESH,
        )
        for j, peer in enumerate(near_peers)
    ]
    for copy in near_copies:
        copy.start()
    for j, peer in enumerate(near_peers):
        slot = lax.rem(near_me + j + 1, group)
        pltpu.make_async_remote_copy(
            src_ref=near_buf.at[slot],
            dst_ref=near_buf.at[slot],
            send_sem=near_send.at[j],
            recv_sem=near_recv.at[slot],
            device_id={"col": peer},
            device_id_type=MESH,
        ).wait_recv()
    total = near_buf[0]
    for slot in range(1, group):
        total = total + near_buf[slot]
    far_buf[far_me] = total
    far_copies = [
        pltpu.make_async_remote_copy(
            src_ref=far_buf.at[far_me],
            dst_ref=far_buf.at[far_me],
            send_sem=far_send.at[j],
            recv_sem=far_recv.at[far_me],
            device_id={"col": peer},
            device_id_type=MESH,
        )
        for j, peer in enumerate(far_peers)
    ]
    for copy in far_copies:
        copy.start()
    for j, peer in enumerate(far_peers):
        slot = lax.rem(far_me + j + 1, far_count)
        pltpu.make_async_remote_copy(
            src_ref=far_buf.at[slot],
            dst_ref=far_buf.at[slot],
            send_sem=far_send.at[j],
            recv_sem=far_recv.at[slot],
            device_id={"col": peer},
            device_id_type=MESH,
        ).wait_recv()
    total = far_buf[0]
    for slot in range(1, far_count):
        total = total + far_buf[slot]
    energy = jnp.sum(jnp.sum(total, axis=1, keepdims=True), axis=0, keepdims=True)
    cells = variables * levels * col_count * count
    root = jnp.sqrt(energy / cells + EPS_ENERGY)
    scale = 1.0 / root
    for v in range(variables):
        for source in range(blocks):
            for part, rows in pieces(v, source):
                out_ref[rows, :] = own[v, part, source * BCOLS : (source + 1) * BCOLS] * scale
    for exchange in range(2):
        for chunk in range(CHUNKS):
            for way in range(2):
                halo_copy(exchange, chunk, way).wait_send()
    for copy in near_copies + far_copies:
        copy.wait_send()


def shards(adj_final, inverses, dep_lists, dep_points, weights):
    variables, levels, col_count = adj_final.shape
    count = lax.axis_size("col")
    blocks = col_count // BCOLS
    padded = -(-levels // 16) * 16
    pairs = blocks // 2
    per_chunk = variables // CHUNKS
    group = min(GROUP, count)
    far_count = count // group
    halo = (2, CHUNKS, 2, per_chunk, padded, PAIR)
    rows = levels * blocks * variables
    like = jax.ShapeDtypeStruct((rows, BCOLS), F32)
    adj_rows = adj_final.reshape(variables, levels, blocks, BCOLS).transpose(1, 2, 0, 3).reshape(rows, BCOLS)
    outs = pl.pallas_call(
        functools.partial(kernel, count),
        out_shape=(like, like),
        in_specs=[pl.BlockSpec(memory_space=pltpu.HBM)] * 5,
        out_specs=(pl.BlockSpec(memory_space=pltpu.VMEM), pl.BlockSpec(memory_space=pltpu.VMEM)),
        scratch_shapes=[
            pltpu.SMEM(dep_lists.shape, jnp.int32),
            pltpu.VMEM(dep_points.shape, jnp.int32),
            pltpu.VMEM(weights.shape, F32),
            pltpu.VMEM((rows, BCOLS), F32),
            pltpu.VMEM((STEPS, blocks, levels, levels), F32),
            pltpu.VMEM((variables, padded, col_count), F32),
            pltpu.VMEM((blocks, padded, padded), F32),
            pltpu.VMEM((STEPS, pairs, WINDOW, PAIR), BF16),
            pltpu.VMEM((STEPS, pairs, WINDOW, PAIR), BF16),
            pltpu.VMEM((variables, padded, col_count), F32),
            pltpu.VMEM(halo, F32),
            pltpu.VMEM(halo, F32),
            pltpu.VMEM((group, 8, BCOLS), F32),
            pltpu.VMEM((far_count, 8, BCOLS), F32),
            pltpu.SemaphoreType.DMA((3,)),
            pltpu.SemaphoreType.DMA((1,)),
            pltpu.SemaphoreType.DMA((STEPS, blocks)),
            pltpu.SemaphoreType.DMA((2, CHUNKS, 2)),
            pltpu.SemaphoreType.DMA((2, CHUNKS, 2)),
            pltpu.SemaphoreType.DMA((group,)),
            pltpu.SemaphoreType.DMA((group,)),
            pltpu.SemaphoreType.DMA((far_count,)),
            pltpu.SemaphoreType.DMA((far_count,)),
        ],
        compiler_params=pltpu.CompilerParams(
            collective_id=0, has_side_effects=True, vmem_limit_bytes=64 << 20
        ),
    )(dep_lists, dep_points, weights, adj_rows, inverses.transpose(0, 2, 1, 3))
    return tuple(
        out.reshape(levels, blocks, variables, BCOLS).transpose(2, 0, 1, 3).reshape(adj_final.shape)
        for out in outs
    )


def solution(mesh):
    in_specs = (
        P("mem", None, "col"),
        P("mem", "col", None, None),
        P("mem", "col", None),
        P("mem", None, "col"),
        P("mem", None, "col"),
    )
    out_specs = (P("mem", None, "col"), P("mem", None, "col"))
    return jax.shard_map(shards, mesh=mesh, in_specs=in_specs, out_specs=out_specs, check_vma=False)
```

```python
import functools

import jax
import jax.numpy as jnp
from jax import lax
from jax.experimental import pallas as pl
from jax.experimental.pallas import tpu as pltpu
from jax.sharding import PartitionSpec as P

BCOLS = 128
REACH = 2
SLOTS = 5
POINTS = 4
STEPS = 2
PAIR = 2 * BCOLS
WINDOW = 3 * PAIR
EPS_ENERGY = 1e-06
GROUP = 8
CHUNKS = 4
MESH = pl.DeviceIdType.MESH
F32 = jnp.float32
BF16 = jnp.bfloat16


def halves(value):
    high = value.astype(BF16)
    low = (value - high.astype(F32)).astype(BF16)
    return high, low


def kernel(
    count,
    lists_hbm,
    points_hbm,
    weights_hbm,
    adj_hbm,
    inv_hbm,
    mid_ref,
    start_ref,
    energy_ref,
    lists_ref,
    points_ref,
    weights_ref,
    adj_in,
    inv_in,
    adj_pad,
    inv_pad,
    w_high,
    w_low,
    own,
    send_buf,
    recv_buf,
    near_buf,
    far_buf,
    small_sem,
    in_sem,
    inv_sem,
    send_sem,
    recv_sem,
    near_send,
    near_recv,
    far_send,
    far_recv,
):
    variables, padded, col_count = adj_pad.shape
    levels = inv_in.shape[-1]
    blocks = col_count // BCOLS
    pairs = blocks // 2
    tiles = pairs + 2
    per_chunk = variables // CHUNKS
    all_blocks = count * blocks
    me = lax.axis_index("col")
    up = lax.rem(me + 1, count)
    down = lax.rem(me + count - 1, count)
    group = min(GROUP, count)
    far_count = count // group
    near_me = lax.rem(me, group)
    far_me = me // group
    near_peers = [far_me * group + lax.rem(near_me + j, group) for j in range(1, group)]
    far_peers = [lax.rem(far_me + j, far_count) * group + near_me for j in range(1, far_count)]

    barrier = pltpu.get_barrier_semaphore()
    everyone = [up, down] + near_peers + far_peers
    for peer in everyone:
        pl.semaphore_signal(barrier, inc=1, device_id={"col": peer}, device_id_type=MESH)

    small_copies = [
        pltpu.make_async_copy(lists_hbm, lists_ref, small_sem.at[0]),
        pltpu.make_async_copy(points_hbm, points_ref, small_sem.at[1]),
        pltpu.make_async_copy(weights_hbm, weights_ref, small_sem.at[2]),
    ]
    inv_copies = {
        step: [
            pltpu.make_async_copy(
                inv_hbm.at[step, :, source, :], inv_in.at[step, source], inv_sem.at[step, source]
            )
            for source in range(blocks)
        ]
        for step in range(STEPS)
    }
    adj_copy = pltpu.make_async_copy(adj_hbm, adj_in, in_sem.at[0])
    for copy in small_copies + inv_copies[1] + [adj_copy] + inv_copies[0]:
        copy.start()

    whole = levels // 8 * 8
    stride = variables * blocks

    def pieces(v, source):
        first = source * variables + v
        yield slice(0, whole), pl.ds(first, whole, stride=stride)
        for level in range(whole, levels):
            yield slice(level, level + 1), pl.ds(level * stride + first, 1)

    def build(step):
        points = points_ref[step]
        slot_ids = points // BCOLS
        within = points % BCOLS
        for source in range(blocks):
            lanes = slice(source * BCOLS, (source + 1) * BCOLS)
            block = me * blocks + source
            slots = slot_ids[:, lanes]
            offset = jnp.zeros_like(slots)
            for slot in range(SLOTS):
                rel = lists_ref[step, source, slot] - block + REACH
                rel = jnp.where(rel < 0, rel + all_blocks, rel)
                rel = jnp.where(rel >= all_blocks, rel - all_blocks, rel)
                offset = jnp.where(slots == slot, rel, offset)
            column = offset * BCOLS + within[:, lanes]
            weight = weights_ref[step][:, lanes]
            parity = source % 2
            pair = source // 2
            half = slice(parity * BCOLS, (parity + 1) * BCOLS)
            empty = jnp.zeros((BCOLS, BCOLS), BF16)
            unused = slice(0, BCOLS) if parity else slice(SLOTS * BCOLS, WINDOW)
            w_high[step, pair, unused, half] = empty
            w_low[step, pair, unused, half] = empty
            for piece in range(SLOTS):
                rows = lax.broadcasted_iota(jnp.int32, (BCOLS, BCOLS), 0) + piece * BCOLS
                total = jnp.zeros((BCOLS, BCOLS), F32)
                for point in range(POINTS):
                    hit = rows == column[point : point + 1]
                    total = total + jnp.where(hit, weight[point : point + 1], 0.0)
                high, low = halves(total)
                place = slice((piece + parity) * BCOLS, (piece + parity + 1) * BCOLS)
                w_high[step, pair, place, half] = high
                w_low[step, pair, place, half] = low

    def pad_inverse(step):
        for source in range(blocks):
            inv_pad[source] = jnp.zeros((padded, padded), F32)
            inv_pad[source, 0:levels, 0:levels] = inv_in[step, source]

    def stacked_inverse(source):
        high, low = halves(inv_pad[source])
        return jnp.concatenate([high, low, high], axis=0)

    def diffuse(inverse, value):
        high, low = halves(value)
        return lax.dot_general(
            inverse,
            jnp.concatenate([high, high, low], axis=0),
            (((0,), (0,)), ((), ())),
            preferred_element_type=F32,
        )

    def diffused_pairs(block_value, inverses):
        result = []
        for pair in range(pairs):
            left = diffuse(inverses[2 * pair], block_value(2 * pair))
            right = diffuse(inverses[2 * pair + 1], block_value(2 * pair + 1))
            rows = [
                jnp.concatenate(
                    [left[:, v * BCOLS : (v + 1) * BCOLS], right[:, v * BCOLS : (v + 1) * BCOLS]], axis=1
                )
                for v in range(per_chunk)
            ]
            result.append(halves(jnp.concatenate(rows, axis=0)))
        return result

    def tile_sum(step, diffused, tile):
        left, right = [], []
        for pair in range(pairs):
            if 0 <= tile - pair <= 2:
                high, low = diffused[pair]
                place = slice((tile - pair) * PAIR, (tile - pair + 1) * PAIR)
                left += [high, low, high]
                matrix = w_high[step, pair, place, :]
                right += [matrix, matrix, w_low[step, pair, place, :]]
        return lax.dot_general(
            jnp.concatenate(left, axis=1),
            jnp.concatenate(right, axis=1),
            (((1,), (1,)), ((), ())),
            preferred_element_type=F32,
        )

    def halo_copy(exchange, chunk, way):
        return pltpu.make_async_remote_copy(
            src_ref=send_buf.at[exchange, chunk, way],
            dst_ref=recv_buf.at[exchange, chunk, way],
            send_sem=send_sem.at[exchange, chunk, way],
            recv_sem=recv_sem.at[exchange, chunk, way],
            device_id={"col": up if way else down},
            device_id_type=MESH,
        )

    def scatter(exchange, step, chunk, diffused, first):
        for way, tile in ((0, 0), (1, tiles - 1)):
            value = tile_sum(step, diffused, tile)
            for v in range(per_chunk):
                send_buf[exchange, chunk, way, v] = value[v * padded : (v + 1) * padded]
        if first:
            pl.semaphore_wait(barrier, len(everyone))
        for way in range(2):
            halo_copy(exchange, chunk, way).start()
        for tile in range(1, tiles - 1):
            value = tile_sum(step, diffused, tile)
            for v in range(per_chunk):
                own[chunk * per_chunk + v, :, (tile - 1) * PAIR : tile * PAIR] = value[
                    v * padded : (v + 1) * padded
                ]

    def arrived(exchange, chunk):
        for way in range(2):
            halo_copy(exchange, chunk, way).wait_recv()
        for v in range(per_chunk):
            row = chunk * per_chunk + v
            own[row, :, 0:PAIR] = own[row, :, 0:PAIR] + recv_buf[exchange, chunk, 1, v]
            last = slice(col_count - PAIR, col_count)
            own[row, :, last] = own[row, :, last] + recv_buf[exchange, chunk, 0, v]

    for copy in small_copies:
        copy.wait()
    build(1)
    for copy in inv_copies[1]:
        copy.wait()
    pad_inverse(1)
    inverses = [stacked_inverse(source) for source in range(blocks)]
    for v in range(variables):
        adj_pad[v, padded - 8 : padded, :] = jnp.zeros((8, col_count), F32)
    for chunk in range(CHUNKS):
        if chunk == 0:
            adj_copy.wait()
        for v in range(chunk * per_chunk, (chunk + 1) * per_chunk):
            for source in range(blocks):
                lanes = slice(source * BCOLS, (source + 1) * BCOLS)
                for part, rows in pieces(v, source):
                    adj_pad[v, part, lanes] = adj_in[rows, :]

        def block_value(source, chunk=chunk):
            lanes = slice(source * BCOLS, (source + 1) * BCOLS)
            return jnp.concatenate(
                [adj_pad[v, :, lanes] for v in range(chunk * per_chunk, (chunk + 1) * per_chunk)], axis=1
            )

        scatter(0, 1, chunk, diffused_pairs(block_value, inverses), chunk == 0)

    build(0)
    for copy in inv_copies[0]:
        copy.wait()
    pad_inverse(0)
    inverses = [stacked_inverse(source) for source in range(blocks)]
    for chunk in range(CHUNKS):
        arrived(0, chunk)
        for v in range(chunk * per_chunk, (chunk + 1) * per_chunk):
            for source in range(blocks):
                for part, rows in pieces(v, source):
                    mid_ref[rows, :] = own[v, part, source * BCOLS : (source + 1) * BCOLS]

        def block_value(source, chunk=chunk):
            lanes = slice(source * BCOLS, (source + 1) * BCOLS)
            return jnp.concatenate(
                [own[v, :, lanes] for v in range(chunk * per_chunk, (chunk + 1) * per_chunk)], axis=1
            )

        scatter(1, 0, chunk, diffused_pairs(block_value, inverses), False)

    total = jnp.zeros((8, BCOLS), F32)
    for chunk in range(CHUNKS):
        arrived(1, chunk)
        for v in range(chunk * per_chunk, (chunk + 1) * per_chunk):
            value = own[v]
            square = value * value
            by_lane = square[:, 0:BCOLS]
            for block in range(1, blocks):
                by_lane = by_lane + square[:, block * BCOLS : (block + 1) * BCOLS]
            total = total + jnp.sum(by_lane.reshape(padded // 8, 8, BCOLS), axis=0)
    total = jnp.sum(total, axis=0, keepdims=True)

    near_buf[near_me] = total
    near_copies = [
        pltpu.make_async_remote_copy(
            src_ref=near_buf.at[near_me],
            dst_ref=near_buf.at[near_me],
            send_sem=near_send.at[j],
            recv_sem=near_recv.at[near_me],
            device_id={"col": peer},
            device_id_type=MESH,
        )
        for j, peer in enumerate(near_peers)
    ]
    for copy in near_copies:
        copy.start()
    for v in range(variables):
        for source in range(blocks):
            for part, rows in pieces(v, source):
                start_ref[rows, :] = own[v, part, source * BCOLS : (source + 1) * BCOLS]
    for j, peer in enumerate(near_peers):
        slot = lax.rem(near_me + j + 1, group)
        pltpu.make_async_remote_copy(
            src_ref=near_buf.at[slot],
            dst_ref=near_buf.at[slot],
            send_sem=near_send.at[j],
            recv_sem=near_recv.at[slot],
            device_id={"col": peer},
            device_id_type=MESH,
        ).wait_recv()
    total = near_buf[0]
    for slot in range(1, group):
        total = total + near_buf[slot]
    far_buf[far_me] = total
    far_copies = [
        pltpu.make_async_remote_copy(
            src_ref=far_buf.at[far_me],
            dst_ref=far_buf.at[far_me],
            send_sem=far_send.at[j],
            recv_sem=far_recv.at[far_me],
            device_id={"col": peer},
            device_id_type=MESH,
        )
        for j, peer in enumerate(far_peers)
    ]
    for copy in far_copies:
        copy.start()
    for j, peer in enumerate(far_peers):
        slot = lax.rem(far_me + j + 1, far_count)
        pltpu.make_async_remote_copy(
            src_ref=far_buf.at[slot],
            dst_ref=far_buf.at[slot],
            send_sem=far_send.at[j],
            recv_sem=far_recv.at[slot],
            device_id={"col": peer},
            device_id_type=MESH,
        ).wait_recv()
    total = far_buf[0]
    for slot in range(1, far_count):
        total = total + far_buf[slot]
    energy_ref[...] = total
    for exchange in range(2):
        for chunk in range(CHUNKS):
            for way in range(2):
                halo_copy(exchange, chunk, way).wait_send()
    for copy in near_copies + far_copies:
        copy.wait_send()


def finish(cells, mid_in, start_in, energy_ref, mid_hbm, out_hbm, scaled, sem):
    mid_copy = pltpu.make_async_copy(mid_in, mid_hbm, sem.at[0])
    mid_copy.start()
    energy = jnp.sum(energy_ref[...], axis=1, keepdims=True)
    scale = 1.0 / jnp.sqrt(energy / cells + EPS_ENERGY)
    scaled[...] = start_in[...] * scale
    out_copy = pltpu.make_async_copy(scaled, out_hbm, sem.at[1])
    out_copy.start()
    mid_copy.wait()
    out_copy.wait()


def shards(adj_final, inverses, dep_lists, dep_points, weights):
    variables, levels, col_count = adj_final.shape
    count = lax.axis_size("col")
    blocks = col_count // BCOLS
    padded = -(-levels // 16) * 16
    pairs = blocks // 2
    per_chunk = variables // CHUNKS
    group = min(GROUP, count)
    far_count = count // group
    halo = (2, CHUNKS, 2, per_chunk, padded, PAIR)
    rows = levels * blocks * variables
    like = jax.ShapeDtypeStruct((rows, BCOLS), F32)
    adj_rows = adj_final.reshape(variables, levels, blocks, BCOLS).transpose(1, 2, 0, 3).reshape(rows, BCOLS)
    vmem = pl.BlockSpec(memory_space=pltpu.VMEM)
    anywhere = pl.BlockSpec(memory_space=pltpu.HBM)
    mid, start, energy = pl.pallas_call(
        functools.partial(kernel, count),
        out_shape=(like, like, jax.ShapeDtypeStruct((1, BCOLS), F32)),
        in_specs=[pl.BlockSpec(memory_space=pltpu.HBM)] * 5,
        out_specs=(vmem, vmem, vmem),
        scratch_shapes=[
            pltpu.SMEM(dep_lists.shape, jnp.int32),
            pltpu.VMEM(dep_points.shape, jnp.int32),
            pltpu.VMEM(weights.shape, F32),
            pltpu.VMEM((rows, BCOLS), F32),
            pltpu.VMEM((STEPS, blocks, levels, levels), F32),
            pltpu.VMEM((variables, padded, col_count), F32),
            pltpu.VMEM((blocks, padded, padded), F32),
            pltpu.VMEM((STEPS, pairs, WINDOW, PAIR), BF16),
            pltpu.VMEM((STEPS, pairs, WINDOW, PAIR), BF16),
            pltpu.VMEM((variables, padded, col_count), F32),
            pltpu.VMEM(halo, F32),
            pltpu.VMEM(halo, F32),
            pltpu.VMEM((group, 1, BCOLS), F32),
            pltpu.VMEM((far_count, 1, BCOLS), F32),
            pltpu.SemaphoreType.DMA((3,)),
            pltpu.SemaphoreType.DMA((1,)),
            pltpu.SemaphoreType.DMA((STEPS, blocks)),
            pltpu.SemaphoreType.DMA((2, CHUNKS, 2)),
            pltpu.SemaphoreType.DMA((2, CHUNKS, 2)),
            pltpu.SemaphoreType.DMA((group,)),
            pltpu.SemaphoreType.DMA((group,)),
            pltpu.SemaphoreType.DMA((far_count,)),
            pltpu.SemaphoreType.DMA((far_count,)),
        ],
        compiler_params=pltpu.CompilerParams(
            collective_id=0, has_side_effects=True, vmem_limit_bytes=48 << 20
        ),
    )(
        *(
            pltpu.with_memory_space_constraint(value, pltpu.HBM)
            for value in (dep_lists, dep_points, weights, adj_rows, inverses.transpose(0, 2, 1, 3))
        )
    )
    outs = pl.pallas_call(
        functools.partial(finish, count * adj_final.size),
        out_shape=(like, like),
        in_specs=[vmem, vmem, vmem],
        out_specs=(anywhere, anywhere),
        scratch_shapes=[pltpu.VMEM((rows, BCOLS), F32), pltpu.SemaphoreType.DMA((2,))],
        compiler_params=pltpu.CompilerParams(vmem_limit_bytes=16 << 20),
    )(mid, start, energy)
    return tuple(
        out.reshape(levels, blocks, variables, BCOLS).transpose(2, 0, 1, 3).reshape(adj_final.shape)
        for out in outs
    )


def solution(mesh):
    in_specs = (
        P("mem", None, "col"),
        P("mem", "col", None, None),
        P("mem", "col", None),
        P("mem", None, "col"),
        P("mem", None, "col"),
    )
    out_specs = (P("mem", None, "col"), P("mem", None, "col"))
    return jax.shard_map(shards, mesh=mesh, in_specs=in_specs, out_specs=out_specs, check_vma=False)
```

```python
import functools

import jax
import jax.numpy as jnp
from jax import lax
from jax.experimental import pallas as pl
from jax.experimental.pallas import tpu as pltpu
from jax.sharding import PartitionSpec as P

BCOLS = 128
REACH = 2
SLOTS = 5
POINTS = 4
STEPS = 2
PAIR = 2 * BCOLS
WINDOW = 3 * PAIR
EPS_ENERGY = 1e-06
GROUP = 8
CHUNKS = 4
MESH = pl.DeviceIdType.MESH
F32 = jnp.float32
BF16 = jnp.bfloat16


def halves(value):
    high = value.astype(BF16)
    low = (value - high.astype(F32)).astype(BF16)
    return high, low


def kernel(
    count,
    lists_hbm,
    points_hbm,
    weights_hbm,
    adj_hbm,
    inv_hbm,
    mid_ref,
    start_ref,
    energy_ref,
    lists_ref,
    points_ref,
    weights_ref,
    adj_in,
    inv_in,
    adj_pad,
    inv_pad,
    w_high,
    w_low,
    own,
    send_buf,
    recv_buf,
    near_buf,
    far_buf,
    line_sem,
    small_sem,
    in_sem,
    inv_sem,
    send_sem,
    recv_sem,
    near_send,
    near_recv,
    far_send,
    far_recv,
):
    variables, padded, col_count = adj_pad.shape
    levels = inv_in.shape[-1]
    blocks = col_count // BCOLS
    pairs = blocks // 2
    tiles = pairs + 2
    per_chunk = variables // CHUNKS
    all_blocks = count * blocks
    me = lax.axis_index("col")
    up = lax.rem(me + 1, count)
    down = lax.rem(me + count - 1, count)
    group = min(GROUP, count)
    far_count = count // group
    near_me = lax.rem(me, group)
    far_me = me // group

    def in_line(distance):
        return lax.rem(far_me + distance + far_count, far_count) * group + near_me

    near_order = sorted(range(1, group), key=lambda j: -min(j, group - j))
    far_order = sorted(range(1, far_count), key=lambda j: -min(j, far_count - j))
    near_peers = [far_me * group + lax.rem(near_me + j, group) for j in near_order]
    far_peers = [in_line(j) for j in far_order]

    barrier = pltpu.get_barrier_semaphore()
    adjacent = [up, down] + near_peers
    if far_count > 1:
        adjacent += [in_line(1), in_line(-1)]
    for peer in adjacent:
        pl.semaphore_signal(barrier, inc=1, device_id={"col": peer}, device_id_type=MESH)

    small_copies = [
        pltpu.make_async_copy(lists_hbm, lists_ref, small_sem.at[0]),
        pltpu.make_async_copy(points_hbm, points_ref, small_sem.at[1]),
        pltpu.make_async_copy(weights_hbm, weights_ref, small_sem.at[2]),
    ]
    inv_copies = {
        step: [
            pltpu.make_async_copy(
                inv_hbm.at[step, :, source, :], inv_in.at[step, source], inv_sem.at[step, source]
            )
            for source in range(blocks)
        ]
        for step in range(STEPS)
    }
    adj_copy = pltpu.make_async_copy(adj_hbm, adj_in, in_sem.at[0])
    for copy in small_copies + inv_copies[1] + [adj_copy] + inv_copies[0]:
        copy.start()

    whole = levels // 8 * 8
    stride = variables * blocks

    def pieces(v, source):
        first = source * variables + v
        yield slice(0, whole), pl.ds(first, whole, stride=stride)
        for level in range(whole, levels):
            yield slice(level, level + 1), pl.ds(level * stride + first, 1)

    reaches = []
    while far_count > 1 and 2 ** len(reaches) < far_count // 2:
        reaches.append(2 ** len(reaches))

    def announce(turn):
        if turn < len(reaches):
            for way, distance in ((0, reaches[turn]), (1, -reaches[turn])):
                pl.semaphore_signal(
                    line_sem.at[turn, way], inc=1, device_id={"col": in_line(distance)}, device_id_type=MESH
                )

    def heard(turn):
        if 0 <= turn < len(reaches):
            for way in range(2):
                pl.semaphore_wait(line_sem.at[turn, way], 1)

    def build(step, first, last):
        points = points_ref[step]
        slot_ids = points // BCOLS
        within = points % BCOLS
        for source in range(blocks):
            lanes = slice(source * BCOLS, (source + 1) * BCOLS)
            block = me * blocks + source
            slots = slot_ids[:, lanes]
            offset = jnp.zeros_like(slots)
            for slot in range(SLOTS):
                rel = lists_ref[step, source, slot] - block + REACH
                rel = jnp.where(rel < 0, rel + all_blocks, rel)
                rel = jnp.where(rel >= all_blocks, rel - all_blocks, rel)
                offset = jnp.where(slots == slot, rel, offset)
            column = offset * BCOLS + within[:, lanes]
            weight = weights_ref[step][:, lanes]
            parity = source % 2
            pair = source // 2
            half = slice(parity * BCOLS, (parity + 1) * BCOLS)
            empty = jnp.zeros((BCOLS, BCOLS), BF16)
            unused = slice(0, BCOLS) if parity else slice(SLOTS * BCOLS, WINDOW)
            if first == 0:
                w_high[step, pair, unused, half] = empty
                w_low[step, pair, unused, half] = empty
            for piece in range(SLOTS):
                if not first <= source + piece <= last and not first <= blocks + 3 - source - piece <= last:
                    continue
                rows = lax.broadcasted_iota(jnp.int32, (BCOLS, BCOLS), 0) + piece * BCOLS
                total = jnp.zeros((BCOLS, BCOLS), F32)
                for point in range(POINTS):
                    hit = rows == column[point : point + 1]
                    total = total + jnp.where(hit, weight[point : point + 1], 0.0)
                high, low = halves(total)
                place = slice((piece + parity) * BCOLS, (piece + parity + 1) * BCOLS)
                w_high[step, pair, place, half] = high
                w_low[step, pair, place, half] = low

    def pad_inverse(step):
        for source in range(blocks):
            inv_pad[source] = jnp.zeros((padded, padded), F32)
            inv_pad[source, 0:levels, 0:levels] = inv_in[step, source]

    def stacked_inverse(source):
        high, low = halves(inv_pad[source])
        return jnp.concatenate([high, low, high], axis=0)

    def diffuse(inverse, value):
        high, low = halves(value)
        return lax.dot_general(
            inverse,
            jnp.concatenate([high, high, low], axis=0),
            (((0,), (0,)), ((), ())),
            preferred_element_type=F32,
        )

    def diffused_pairs(block_value, inverses):
        result = []
        for pair in range(pairs):
            left = diffuse(inverses[2 * pair], block_value(2 * pair))
            right = diffuse(inverses[2 * pair + 1], block_value(2 * pair + 1))
            rows = [
                jnp.concatenate(
                    [left[:, v * BCOLS : (v + 1) * BCOLS], right[:, v * BCOLS : (v + 1) * BCOLS]], axis=1
                )
                for v in range(per_chunk)
            ]
            result.append(halves(jnp.concatenate(rows, axis=0)))
        return result

    def tile_sum(step, diffused, tile):
        left, right = [], []
        for pair in range(pairs):
            if 0 <= tile - pair <= 2:
                high, low = diffused[pair]
                place = slice((tile - pair) * PAIR, (tile - pair + 1) * PAIR)
                left += [high, low, high]
                matrix = w_high[step, pair, place, :]
                right += [matrix, matrix, w_low[step, pair, place, :]]
        return lax.dot_general(
            jnp.concatenate(left, axis=1),
            jnp.concatenate(right, axis=1),
            (((1,), (1,)), ((), ())),
            preferred_element_type=F32,
        )

    def halo_copy(exchange, chunk, way):
        return pltpu.make_async_remote_copy(
            src_ref=send_buf.at[exchange, chunk, way],
            dst_ref=recv_buf.at[exchange, chunk, way],
            send_sem=send_sem.at[exchange, chunk, way],
            recv_sem=recv_sem.at[exchange, chunk, way],
            device_id={"col": up if way else down},
            device_id_type=MESH,
        )

    def scatter(exchange, step, chunk, diffused, first):
        for way, tile in ((0, 0), (1, tiles - 1)):
            value = tile_sum(step, diffused, tile)
            for v in range(per_chunk):
                send_buf[exchange, chunk, way, v] = value[v * padded : v * padded + levels]
        if first:
            pl.semaphore_wait(barrier, len(adjacent))
        for way in range(2):
            halo_copy(exchange, chunk, way).start()
        if first:
            announce(0)
            build(1, 2, 3)
        for tile in range(1, tiles - 1):
            value = tile_sum(step, diffused, tile)
            for v in range(per_chunk):
                own[chunk * per_chunk + v, :, (tile - 1) * PAIR : tile * PAIR] = value[
                    v * padded : (v + 1) * padded
                ]

    def arrived(exchange, chunk):
        for way in range(2):
            halo_copy(exchange, chunk, way).wait_recv()
        for v in range(per_chunk):
            row = chunk * per_chunk + v
            part = slice(0, levels)
            own[row, part, 0:PAIR] = own[row, part, 0:PAIR] + recv_buf[exchange, chunk, 1, v]
            last = slice(col_count - PAIR, col_count)
            own[row, part, last] = own[row, part, last] + recv_buf[exchange, chunk, 0, v]

    for copy in small_copies:
        copy.wait()
    build(1, 0, 1)
    for copy in inv_copies[1]:
        copy.wait()
    pad_inverse(1)
    inverses = [stacked_inverse(source) for source in range(blocks)]
    for v in range(variables):
        adj_pad[v, padded - 8 : padded, :] = jnp.zeros((8, col_count), F32)
    for chunk in range(CHUNKS):
        if chunk == 0:
            adj_copy.wait()
        for v in range(chunk * per_chunk, (chunk + 1) * per_chunk):
            for source in range(blocks):
                lanes = slice(source * BCOLS, (source + 1) * BCOLS)
                for part, rows in pieces(v, source):
                    adj_pad[v, part, lanes] = adj_in[rows, :]

        def block_value(source, chunk=chunk):
            lanes = slice(source * BCOLS, (source + 1) * BCOLS)
            return jnp.concatenate(
                [adj_pad[v, :, lanes] for v in range(chunk * per_chunk, (chunk + 1) * per_chunk)], axis=1
            )

        scatter(0, 1, chunk, diffused_pairs(block_value, inverses), chunk == 0)

    build(0, 0, 1)
    build(0, 2, 3)
    for copy in inv_copies[0]:
        copy.wait()
    pad_inverse(0)
    inverses = [stacked_inverse(source) for source in range(blocks)]
    for chunk in range(CHUNKS):
        arrived(0, chunk)
        heard(chunk)
        announce(chunk + 1)
        for v in range(chunk * per_chunk, (chunk + 1) * per_chunk):
            for source in range(blocks):
                for part, rows in pieces(v, source):
                    mid_ref[rows, :] = own[v, part, source * BCOLS : (source + 1) * BCOLS]

        def block_value(source, chunk=chunk):
            lanes = slice(source * BCOLS, (source + 1) * BCOLS)
            return jnp.concatenate(
                [own[v, :, lanes] for v in range(chunk * per_chunk, (chunk + 1) * per_chunk)], axis=1
            )

        scatter(1, 0, chunk, diffused_pairs(block_value, inverses), False)

    total = jnp.zeros((8, BCOLS), F32)
    for chunk in range(CHUNKS):
        arrived(1, chunk)
        if chunk == 0:
            for turn in range(CHUNKS, len(reaches)):
                heard(turn)
                announce(turn + 1)
        for v in range(chunk * per_chunk, (chunk + 1) * per_chunk):
            value = own[v]
            square = value * value
            by_lane = square[:, 0:BCOLS]
            for block in range(1, blocks):
                by_lane = by_lane + square[:, block * BCOLS : (block + 1) * BCOLS]
            total = total + jnp.sum(by_lane.reshape(padded // 8, 8, BCOLS), axis=0)
    total = jnp.sum(total, axis=0, keepdims=True)

    near_buf[near_me] = total
    near_copies = [
        pltpu.make_async_remote_copy(
            src_ref=near_buf.at[near_me],
            dst_ref=near_buf.at[near_me],
            send_sem=near_send.at[j],
            recv_sem=near_recv.at[near_me],
            device_id={"col": peer},
            device_id_type=MESH,
        )
        for j, peer in enumerate(near_peers)
    ]
    for copy in near_copies:
        copy.start()
    for v in range(variables):
        for source in range(blocks):
            for part, rows in pieces(v, source):
                start_ref[rows, :] = own[v, part, source * BCOLS : (source + 1) * BCOLS]
    for j, peer in reversed(list(enumerate(near_peers))):
        slot = lax.rem(near_me + near_order[j], group)
        pltpu.make_async_remote_copy(
            src_ref=near_buf.at[slot],
            dst_ref=near_buf.at[slot],
            send_sem=near_send.at[j],
            recv_sem=near_recv.at[slot],
            device_id={"col": peer},
            device_id_type=MESH,
        ).wait_recv()
    total = near_buf[0]
    for slot in range(1, group):
        total = total + near_buf[slot]
    far_buf[far_me] = total
    far_copies = [
        pltpu.make_async_remote_copy(
            src_ref=far_buf.at[far_me],
            dst_ref=far_buf.at[far_me],
            send_sem=far_send.at[j],
            recv_sem=far_recv.at[far_me],
            device_id={"col": peer},
            device_id_type=MESH,
        )
        for j, peer in enumerate(far_peers)
    ]
    for copy in far_copies:
        copy.start()
    for j, peer in reversed(list(enumerate(far_peers))):
        slot = lax.rem(far_me + far_order[j], far_count)
        pltpu.make_async_remote_copy(
            src_ref=far_buf.at[slot],
            dst_ref=far_buf.at[slot],
            send_sem=far_send.at[j],
            recv_sem=far_recv.at[slot],
            device_id={"col": peer},
            device_id_type=MESH,
        ).wait_recv()
    total = far_buf[0]
    for slot in range(1, far_count):
        total = total + far_buf[slot]
    energy_ref[...] = total
    for exchange in range(2):
        for chunk in range(CHUNKS):
            for way in range(2):
                halo_copy(exchange, chunk, way).wait_send()
    for copy in near_copies + far_copies:
        copy.wait_send()


def finish(cells, mid_in, start_in, energy_ref, mid_hbm, out_hbm, scaled, sem):
    mid_copy = pltpu.make_async_copy(mid_in, mid_hbm, sem.at[0])
    mid_copy.start()
    energy = jnp.sum(energy_ref[...], axis=1, keepdims=True)
    scale = 1.0 / jnp.sqrt(energy / cells + EPS_ENERGY)
    scaled[...] = start_in[...] * scale
    out_copy = pltpu.make_async_copy(scaled, out_hbm, sem.at[1])
    out_copy.start()
    mid_copy.wait()
    out_copy.wait()


def shards(adj_final, inverses, dep_lists, dep_points, weights):
    variables, levels, col_count = adj_final.shape
    count = lax.axis_size("col")
    blocks = col_count // BCOLS
    padded = -(-levels // 16) * 16
    pairs = blocks // 2
    per_chunk = variables // CHUNKS
    group = min(GROUP, count)
    far_count = count // group
    halo = (2, CHUNKS, 2, per_chunk, levels, PAIR)
    rows = levels * blocks * variables
    like = jax.ShapeDtypeStruct((rows, BCOLS), F32)
    adj_rows = adj_final.reshape(variables, levels, blocks, BCOLS).transpose(1, 2, 0, 3).reshape(rows, BCOLS)
    vmem = pl.BlockSpec(memory_space=pltpu.VMEM)
    anywhere = pl.BlockSpec(memory_space=pltpu.HBM)
    mid, start, energy = pl.pallas_call(
        functools.partial(kernel, count),
        out_shape=(like, like, jax.ShapeDtypeStruct((1, BCOLS), F32)),
        in_specs=[pl.BlockSpec(memory_space=pltpu.HBM)] * 5,
        out_specs=(vmem, vmem, vmem),
        scratch_shapes=[
            pltpu.SMEM(dep_lists.shape, jnp.int32),
            pltpu.VMEM(dep_points.shape, jnp.int32),
            pltpu.VMEM(weights.shape, F32),
            pltpu.VMEM((rows, BCOLS), F32),
            pltpu.VMEM((STEPS, blocks, levels, levels), F32),
            pltpu.VMEM((variables, padded, col_count), F32),
            pltpu.VMEM((blocks, padded, padded), F32),
            pltpu.VMEM((STEPS, pairs, WINDOW, PAIR), BF16),
            pltpu.VMEM((STEPS, pairs, WINDOW, PAIR), BF16),
            pltpu.VMEM((variables, padded, col_count), F32),
            pltpu.VMEM(halo, F32),
            pltpu.VMEM(halo, F32),
            pltpu.VMEM((group, 1, BCOLS), F32),
            pltpu.VMEM((far_count, 1, BCOLS), F32),
            pltpu.SemaphoreType.REGULAR((8, 2)),
            pltpu.SemaphoreType.DMA((3,)),
            pltpu.SemaphoreType.DMA((1,)),
            pltpu.SemaphoreType.DMA((STEPS, blocks)),
            pltpu.SemaphoreType.DMA((2, CHUNKS, 2)),
            pltpu.SemaphoreType.DMA((2, CHUNKS, 2)),
            pltpu.SemaphoreType.DMA((group,)),
            pltpu.SemaphoreType.DMA((group,)),
            pltpu.SemaphoreType.DMA((far_count,)),
            pltpu.SemaphoreType.DMA((far_count,)),
        ],
        compiler_params=pltpu.CompilerParams(
            collective_id=0, has_side_effects=True, vmem_limit_bytes=48 << 20
        ),
    )(
        *(
            pltpu.with_memory_space_constraint(value, pltpu.HBM)
            for value in (dep_lists, dep_points, weights, adj_rows, inverses.transpose(0, 2, 1, 3))
        )
    )
    outs = pl.pallas_call(
        functools.partial(finish, count * adj_final.size),
        out_shape=(like, like),
        in_specs=[vmem, vmem, vmem],
        out_specs=(anywhere, anywhere),
        scratch_shapes=[pltpu.VMEM((rows, BCOLS), F32), pltpu.SemaphoreType.DMA((2,))],
        compiler_params=pltpu.CompilerParams(vmem_limit_bytes=16 << 20),
    )(mid, start, energy)
    return tuple(
        out.reshape(levels, blocks, variables, BCOLS).transpose(2, 0, 1, 3).reshape(adj_final.shape)
        for out in outs
    )


def solution(mesh):
    in_specs = (
        P("mem", None, "col"),
        P("mem", "col", None, None),
        P("mem", "col", None),
        P("mem", None, "col"),
        P("mem", None, "col"),
    )
    out_specs = (P("mem", None, "col"), P("mem", None, "col"))
    return jax.shard_map(shards, mesh=mesh, in_specs=in_specs, out_specs=out_specs, check_vma=False)
```

```python
import functools

import jax
import jax.numpy as jnp
from jax import lax
from jax.experimental import pallas as pl
from jax.experimental.pallas import tpu as pltpu
from jax.sharding import PartitionSpec as P

BCOLS = 128
REACH = 2
SLOTS = 5
POINTS = 4
STEPS = 2
PAIR = 2 * BCOLS
WINDOW = 3 * PAIR
EPS_ENERGY = 1e-06
GROUP = 8
CHUNKS = 4
FINISH_PARTS = 1
MESH = pl.DeviceIdType.MESH
F32 = jnp.float32
BF16 = jnp.bfloat16


def halves(value):
    high = value.astype(BF16)
    low = (value - high.astype(F32)).astype(BF16)
    return high, low


def kernel(
    count,
    lists_hbm,
    points_hbm,
    weights_hbm,
    adj_hbm,
    inv_hbm,
    mid_ref,
    start_ref,
    energy_ref,
    lists_ref,
    points_ref,
    weights_ref,
    adj_in,
    inv_in,
    adj_pad,
    inv_pad,
    w_high,
    w_low,
    own,
    send_buf,
    recv_buf,
    near_buf,
    far_buf,
    line_sem,
    small_sem,
    in_sem,
    inv_sem,
    send_sem,
    recv_sem,
    near_send,
    near_recv,
    far_send,
    far_recv,
):
    variables, padded, col_count = adj_pad.shape
    levels = inv_in.shape[-1]
    blocks = col_count // BCOLS
    pairs = blocks // 2
    tiles = pairs + 2
    per_chunk = variables // CHUNKS
    all_blocks = count * blocks
    me = lax.axis_index("col")
    up = lax.rem(me + 1, count)
    down = lax.rem(me + count - 1, count)
    group = min(GROUP, count)
    far_count = count // group
    near_me = lax.rem(me, group)
    far_me = me // group

    def in_line(distance):
        return lax.rem(far_me + distance + far_count, far_count) * group + near_me

    near_order = sorted(range(1, group), key=lambda j: -min(j, group - j))
    far_order = sorted(range(1, far_count), key=lambda j: -min(j, far_count - j))
    near_peers = [far_me * group + lax.rem(near_me + j, group) for j in near_order]
    far_peers = [in_line(j) for j in far_order]

    barrier = pltpu.get_barrier_semaphore()
    adjacent = [up, down] + near_peers
    if far_count > 1:
        adjacent += [in_line(1), in_line(-1)]
    for peer in adjacent:
        pl.semaphore_signal(barrier, inc=1, device_id={"col": peer}, device_id_type=MESH)

    small_copies = [
        pltpu.make_async_copy(lists_hbm, lists_ref, small_sem.at[0]),
        pltpu.make_async_copy(points_hbm, points_ref, small_sem.at[1]),
        pltpu.make_async_copy(weights_hbm, weights_ref, small_sem.at[2]),
    ]
    inv_copies = {
        step: [
            pltpu.make_async_copy(
                inv_hbm.at[step, :, source, :], inv_in.at[step, source], inv_sem.at[step, source]
            )
            for source in range(blocks)
        ]
        for step in range(STEPS)
    }
    adj_copy = pltpu.make_async_copy(adj_hbm, adj_in, in_sem.at[0])
    for copy in small_copies + inv_copies[1] + [adj_copy] + inv_copies[0]:
        copy.start()

    whole = levels // 8 * 8
    stride = variables * blocks

    def pieces(v, source):
        first = source * variables + v
        yield slice(0, whole), pl.ds(first, whole, stride=stride)
        for level in range(whole, levels):
            yield slice(level, level + 1), pl.ds(level * stride + first, 1)

    reaches = []
    while far_count > 1 and 2 ** len(reaches) < far_count // 2:
        reaches.append(2 ** len(reaches))

    def announce(turn):
        if turn < len(reaches):
            for way, distance in ((0, reaches[turn]), (1, -reaches[turn])):
                pl.semaphore_signal(
                    line_sem.at[turn, way], inc=1, device_id={"col": in_line(distance)}, device_id_type=MESH
                )

    def heard(turn):
        if 0 <= turn < len(reaches):
            for way in range(2):
                pl.semaphore_wait(line_sem.at[turn, way], 1)

    def build(step, first, last):
        points = points_ref[step]
        slot_ids = points // BCOLS
        within = points % BCOLS
        for source in range(blocks):
            lanes = slice(source * BCOLS, (source + 1) * BCOLS)
            block = me * blocks + source
            slots = slot_ids[:, lanes]
            offset = jnp.zeros_like(slots)
            for slot in range(SLOTS):
                rel = lists_ref[step, source, slot] - block + REACH
                rel = jnp.where(rel < 0, rel + all_blocks, rel)
                rel = jnp.where(rel >= all_blocks, rel - all_blocks, rel)
                offset = jnp.where(slots == slot, rel, offset)
            column = offset * BCOLS + within[:, lanes]
            weight = weights_ref[step][:, lanes]
            parity = source % 2
            pair = source // 2
            half = slice(parity * BCOLS, (parity + 1) * BCOLS)
            empty = jnp.zeros((BCOLS, BCOLS), BF16)
            unused = slice(0, BCOLS) if parity else slice(SLOTS * BCOLS, WINDOW)
            if first == 0:
                w_high[step, pair, unused, half] = empty
                w_low[step, pair, unused, half] = empty
            for piece in range(SLOTS):
                if not first <= source + piece <= last and not first <= blocks + 3 - source - piece <= last:
                    continue
                rows = lax.broadcasted_iota(jnp.int32, (BCOLS, BCOLS), 0) + piece * BCOLS
                total = jnp.zeros((BCOLS, BCOLS), F32)
                for point in range(POINTS):
                    hit = rows == column[point : point + 1]
                    total = total + jnp.where(hit, weight[point : point + 1], 0.0)
                high, low = halves(total)
                place = slice((piece + parity) * BCOLS, (piece + parity + 1) * BCOLS)
                w_high[step, pair, place, half] = high
                w_low[step, pair, place, half] = low

    def pad_inverse(step):
        for source in range(blocks):
            inv_pad[source] = jnp.zeros((padded, padded), F32)
            inv_pad[source, 0:levels, 0:levels] = inv_in[step, source]

    def stacked_inverse(source):
        high, low = halves(inv_pad[source])
        return jnp.concatenate([high, low, high], axis=0)

    def diffuse(inverse, value):
        high, low = halves(value)
        return lax.dot_general(
            inverse,
            jnp.concatenate([high, high, low], axis=0),
            (((0,), (0,)), ((), ())),
            preferred_element_type=F32,
        )

    def diffused_pairs(block_value, inverses):
        result = []
        for pair in range(pairs):
            left = diffuse(inverses[2 * pair], block_value(2 * pair))
            right = diffuse(inverses[2 * pair + 1], block_value(2 * pair + 1))
            rows = [
                jnp.concatenate(
                    [left[:, v * BCOLS : (v + 1) * BCOLS], right[:, v * BCOLS : (v + 1) * BCOLS]], axis=1
                )
                for v in range(per_chunk)
            ]
            result.append(halves(jnp.concatenate(rows, axis=0)))
        return result

    def tile_sum(step, diffused, tile):
        left, right = [], []
        for pair in range(pairs):
            if 0 <= tile - pair <= 2:
                high, low = diffused[pair]
                place = slice((tile - pair) * PAIR, (tile - pair + 1) * PAIR)
                left += [high, low, high]
                matrix = w_high[step, pair, place, :]
                right += [matrix, matrix, w_low[step, pair, place, :]]
        return lax.dot_general(
            jnp.concatenate(left, axis=1),
            jnp.concatenate(right, axis=1),
            (((1,), (1,)), ((), ())),
            preferred_element_type=F32,
        )

    def halo_copy(exchange, chunk, way):
        return pltpu.make_async_remote_copy(
            src_ref=send_buf.at[exchange, chunk, way],
            dst_ref=recv_buf.at[exchange, chunk, way],
            send_sem=send_sem.at[exchange, chunk, way],
            recv_sem=recv_sem.at[exchange, chunk, way],
            device_id={"col": up if way else down},
            device_id_type=MESH,
        )

    def scatter(exchange, step, chunk, diffused, first, between):
        for way, tile in ((0, 0), (1, tiles - 1)):
            value = tile_sum(step, diffused, tile)
            for v in range(per_chunk):
                send_buf[exchange, chunk, way, v] = value[v * padded : v * padded + levels]
        if first:
            pl.semaphore_wait(barrier, len(adjacent))
        for way in range(2):
            halo_copy(exchange, chunk, way).start()
        between()
        for tile in range(1, tiles - 1):
            value = tile_sum(step, diffused, tile)
            for v in range(per_chunk):
                own[chunk * per_chunk + v, :, (tile - 1) * PAIR : tile * PAIR] = value[
                    v * padded : (v + 1) * padded
                ]

    def arrived(exchange, chunk):
        for way in range(2):
            halo_copy(exchange, chunk, way).wait_recv()
        for v in range(per_chunk):
            row = chunk * per_chunk + v
            part = slice(0, levels)
            own[row, part, 0:PAIR] = own[row, part, 0:PAIR] + recv_buf[exchange, chunk, 1, v]
            last = slice(col_count - PAIR, col_count)
            own[row, part, last] = own[row, part, last] + recv_buf[exchange, chunk, 0, v]

    for copy in small_copies:
        copy.wait()
    build(1, 0, 1)
    for copy in inv_copies[1]:
        copy.wait()
    pad_inverse(1)
    inverses = [stacked_inverse(source) for source in range(blocks)]
    for v in range(variables):
        adj_pad[v, padded - 8 : padded, :] = jnp.zeros((8, col_count), F32)
    for chunk in range(CHUNKS):
        if chunk == 0:
            adj_copy.wait()
        for v in range(chunk * per_chunk, (chunk + 1) * per_chunk):
            for source in range(blocks):
                lanes = slice(source * BCOLS, (source + 1) * BCOLS)
                for part, rows in pieces(v, source):
                    adj_pad[v, part, lanes] = adj_in[rows, :]

        def block_value(source, chunk=chunk):
            lanes = slice(source * BCOLS, (source + 1) * BCOLS)
            return jnp.concatenate(
                [adj_pad[v, :, lanes] for v in range(chunk * per_chunk, (chunk + 1) * per_chunk)], axis=1
            )

        def rest_of_weights(chunk=chunk):
            if chunk == 0:
                announce(0)
                build(1, 2, 3)

        scatter(0, 1, chunk, diffused_pairs(block_value, inverses), chunk == 0, rest_of_weights)

    build(0, 0, 1)
    build(0, 2, 3)
    for copy in inv_copies[0]:
        copy.wait()
    pad_inverse(0)
    inverses = [stacked_inverse(source) for source in range(blocks)]
    heard(0)
    announce(1)
    for chunk in range(CHUNKS):
        arrived(0, chunk)
        def block_value(source, chunk=chunk):
            lanes = slice(source * BCOLS, (source + 1) * BCOLS)
            return jnp.concatenate(
                [own[v, :, lanes] for v in range(chunk * per_chunk, (chunk + 1) * per_chunk)], axis=1
            )

        def keep_mid(chunk=chunk):
            for v in range(chunk * per_chunk, (chunk + 1) * per_chunk):
                for source in range(blocks):
                    for part, rows in pieces(v, source):
                        mid_ref[rows, :] = own[v, part, source * BCOLS : (source + 1) * BCOLS]

        scatter(1, 0, chunk, diffused_pairs(block_value, inverses), False, keep_mid)
        if chunk == 1:
            heard(1)
            announce(2)

    total = jnp.zeros((8, BCOLS), F32)
    for chunk in range(CHUNKS):
        arrived(1, chunk)
        for v in range(chunk * per_chunk, (chunk + 1) * per_chunk):
            value = own[v]
            square = value * value
            by_lane = square[:, 0:BCOLS]
            for block in range(1, blocks):
                by_lane = by_lane + square[:, block * BCOLS : (block + 1) * BCOLS]
            total = total + jnp.sum(by_lane.reshape(padded // 8, 8, BCOLS), axis=0)
    total = jnp.sum(total, axis=0, keepdims=True)

    near_buf[near_me] = total
    near_copies = [
        pltpu.make_async_remote_copy(
            src_ref=near_buf.at[near_me],
            dst_ref=near_buf.at[near_me],
            send_sem=near_send.at[j],
            recv_sem=near_recv.at[0],
            device_id={"col": peer},
            device_id_type=MESH,
        )
        for j, peer in enumerate(near_peers)
    ]
    for copy in near_copies:
        copy.start()
    for v in range(variables):
        for source in range(blocks):
            for part, rows in pieces(v, source):
                start_ref[rows, :] = own[v, part, source * BCOLS : (source + 1) * BCOLS]
    if group > 1:
        others = pl.ds(0, group - 1)
        pltpu.make_async_remote_copy(
            src_ref=near_buf.at[others],
            dst_ref=near_buf.at[others],
            send_sem=near_send.at[0],
            recv_sem=near_recv.at[0],
            device_id={"col": near_peers[0]},
            device_id_type=MESH,
        ).wait_recv()
    total = jnp.sum(near_buf[...], axis=0)
    far_buf[far_me] = total
    far_copies = [
        pltpu.make_async_remote_copy(
            src_ref=far_buf.at[far_me],
            dst_ref=far_buf.at[far_me],
            send_sem=far_send.at[j],
            recv_sem=far_recv.at[0],
            device_id={"col": peer},
            device_id_type=MESH,
        )
        for j, peer in enumerate(far_peers)
    ]
    for turn in range(2, len(reaches)):
        heard(turn)
        announce(turn + 1)
    for copy in far_copies:
        copy.start()
    if far_count > 1:
        others = pl.ds(0, far_count - 1)
        pltpu.make_async_remote_copy(
            src_ref=far_buf.at[others],
            dst_ref=far_buf.at[others],
            send_sem=far_send.at[0],
            recv_sem=far_recv.at[0],
            device_id={"col": far_peers[0]},
            device_id_type=MESH,
        ).wait_recv()
    total = jnp.sum(far_buf[...], axis=0)
    energy_ref[...] = total
    for exchange in range(2):
        for chunk in range(CHUNKS):
            for way in range(2):
                halo_copy(exchange, chunk, way).wait_send()
    for copy in near_copies + far_copies:
        copy.wait_send()


def finish(cells, mid_in, start_in, energy_ref, mid_hbm, out_hbm, scaled, sem):
    mid_copy = pltpu.make_async_copy(mid_in, mid_hbm, sem.at[0])
    mid_copy.start()
    energy = jnp.sum(energy_ref[...], axis=1, keepdims=True)
    scale = 1.0 / jnp.sqrt(energy / cells + EPS_ENERGY)
    size = scaled.shape[0] // FINISH_PARTS
    copies = [mid_copy]
    for piece in range(FINISH_PARTS):
        part = pl.ds(piece * size, size)
        scaled[part, :] = start_in[part, :] * scale
        copy = pltpu.make_async_copy(scaled.at[part], out_hbm.at[part], sem.at[1 + piece])
        copy.start()
        copies.append(copy)
    for copy in copies:
        copy.wait()


def shards(adj_final, inverses, dep_lists, dep_points, weights):
    variables, levels, col_count = adj_final.shape
    count = lax.axis_size("col")
    blocks = col_count // BCOLS
    padded = -(-levels // 16) * 16
    pairs = blocks // 2
    per_chunk = variables // CHUNKS
    group = min(GROUP, count)
    far_count = count // group
    halo = (2, CHUNKS, 2, per_chunk, levels, PAIR)
    rows = levels * blocks * variables
    like = jax.ShapeDtypeStruct((rows, BCOLS), F32)
    adj_rows = adj_final.reshape(variables, levels, blocks, BCOLS).transpose(1, 2, 0, 3).reshape(rows, BCOLS)
    vmem = pl.BlockSpec(memory_space=pltpu.VMEM)
    anywhere = pl.BlockSpec(memory_space=pltpu.HBM)
    mid, start, energy = pl.pallas_call(
        functools.partial(kernel, count),
        out_shape=(like, like, jax.ShapeDtypeStruct((1, BCOLS), F32)),
        in_specs=[pl.BlockSpec(memory_space=pltpu.HBM)] * 5,
        out_specs=(vmem, vmem, vmem),
        scratch_shapes=[
            pltpu.SMEM(dep_lists.shape, jnp.int32),
            pltpu.VMEM(dep_points.shape, jnp.int32),
            pltpu.VMEM(weights.shape, F32),
            pltpu.VMEM((rows, BCOLS), F32),
            pltpu.VMEM((STEPS, blocks, levels, levels), F32),
            pltpu.VMEM((variables, padded, col_count), F32),
            pltpu.VMEM((blocks, padded, padded), F32),
            pltpu.VMEM((STEPS, pairs, WINDOW, PAIR), BF16),
            pltpu.VMEM((STEPS, pairs, WINDOW, PAIR), BF16),
            pltpu.VMEM((variables, padded, col_count), F32),
            pltpu.VMEM(halo, F32),
            pltpu.VMEM(halo, F32),
            pltpu.VMEM((group, 1, BCOLS), F32),
            pltpu.VMEM((far_count, 1, BCOLS), F32),
            pltpu.SemaphoreType.REGULAR((8, 2)),
            pltpu.SemaphoreType.DMA((3,)),
            pltpu.SemaphoreType.DMA((1,)),
            pltpu.SemaphoreType.DMA((STEPS, blocks)),
            pltpu.SemaphoreType.DMA((2, CHUNKS, 2)),
            pltpu.SemaphoreType.DMA((2, CHUNKS, 2)),
            pltpu.SemaphoreType.DMA((group,)),
            pltpu.SemaphoreType.DMA((group,)),
            pltpu.SemaphoreType.DMA((far_count,)),
            pltpu.SemaphoreType.DMA((far_count,)),
        ],
        compiler_params=pltpu.CompilerParams(
            collective_id=0, has_side_effects=True, vmem_limit_bytes=48 << 20
        ),
    )(
        *(
            pltpu.with_memory_space_constraint(value, pltpu.HBM)
            for value in (dep_lists, dep_points, weights, adj_rows, inverses.transpose(0, 2, 1, 3))
        )
    )
    outs = pl.pallas_call(
        functools.partial(finish, count * adj_final.size),
        out_shape=(like, like),
        in_specs=[vmem, vmem, vmem],
        out_specs=(anywhere, anywhere),
        scratch_shapes=[pltpu.VMEM((rows, BCOLS), F32), pltpu.SemaphoreType.DMA((1 + FINISH_PARTS,))],
        compiler_params=pltpu.CompilerParams(vmem_limit_bytes=16 << 20),
    )(mid, start, energy)
    return tuple(
        out.reshape(levels, blocks, variables, BCOLS).transpose(2, 0, 1, 3).reshape(adj_final.shape)
        for out in outs
    )


def solution(mesh):
    in_specs = (
        P("mem", None, "col"),
        P("mem", "col", None, None),
        P("mem", "col", None),
        P("mem", None, "col"),
        P("mem", None, "col"),
    )
    out_specs = (P("mem", None, "col"), P("mem", None, "col"))
    return jax.shard_map(shards, mesh=mesh, in_specs=in_specs, out_specs=out_specs, check_vma=False)
```

```python
import functools

import jax
import jax.numpy as jnp
from jax import lax
from jax.experimental import pallas as pl
from jax.experimental.pallas import tpu as pltpu
from jax.sharding import PartitionSpec as P

BCOLS = 128
REACH = 2
SLOTS = 5
POINTS = 4
STEPS = 2
PAIR = 2 * BCOLS
WINDOW = 3 * PAIR
EPS_ENERGY = 1e-06
GROUP = 8
CHUNKS = 4
FINISH_PARTS = 1
MESH = pl.DeviceIdType.MESH
F32 = jnp.float32
BF16 = jnp.bfloat16


def halves(value):
    high = value.astype(BF16)
    low = (value - high.astype(F32)).astype(BF16)
    return high, low


def kernel(
    count,
    lists_hbm,
    points_hbm,
    weights_hbm,
    adj_hbm,
    inv_hbm,
    mid_ref,
    start_ref,
    energy_ref,
    lists_ref,
    points_ref,
    weights_ref,
    adj_in,
    inv_in,
    adj_pad,
    inv_pad,
    w_high,
    w_low,
    own,
    send_buf,
    recv_buf,
    near_buf,
    far_buf,
    line_sem,
    small_sem,
    in_sem,
    inv_sem,
    send_sem,
    recv_sem,
    near_send,
    near_recv,
    far_send,
    far_recv,
):
    variables, padded, col_count = adj_pad.shape
    levels = inv_in.shape[-1]
    blocks = col_count // BCOLS
    pairs = blocks // 2
    tiles = pairs + 2
    per_chunk = variables // CHUNKS
    all_blocks = count * blocks
    me = lax.axis_index("col")
    up = lax.rem(me + 1, count)
    down = lax.rem(me + count - 1, count)
    group = min(GROUP, count)
    far_count = count // group
    near_me = lax.rem(me, group)
    far_me = me // group

    def in_line(distance):
        return lax.rem(far_me + distance + far_count, far_count) * group + near_me

    near_order = sorted(range(1, group), key=lambda j: -min(j, group - j))
    far_order = sorted(range(1, far_count), key=lambda j: -min(j, far_count - j))
    near_peers = [far_me * group + lax.rem(near_me + j, group) for j in near_order]
    far_peers = [in_line(j) for j in far_order]

    barrier = pltpu.get_barrier_semaphore()
    adjacent = [up, down] + near_peers
    if far_count > 1:
        adjacent += [in_line(1), in_line(-1)]
    for peer in adjacent:
        pl.semaphore_signal(barrier, inc=1, device_id={"col": peer}, device_id_type=MESH)

    small_copies = [
        pltpu.make_async_copy(lists_hbm, lists_ref, small_sem.at[0]),
        pltpu.make_async_copy(points_hbm, points_ref, small_sem.at[1]),
        pltpu.make_async_copy(weights_hbm, weights_ref, small_sem.at[2]),
    ]
    inv_copies = {
        step: [
            pltpu.make_async_copy(
                inv_hbm.at[step, :, source, :], inv_in.at[step, source], inv_sem.at[step, source]
            )
            for source in range(blocks)
        ]
        for step in range(STEPS)
    }
    adj_copy = pltpu.make_async_copy(adj_hbm, adj_in, in_sem.at[0])
    for copy in small_copies + inv_copies[1] + [adj_copy] + inv_copies[0]:
        copy.start()

    whole = levels // 8 * 8
    stride = variables * blocks

    def pieces(v, source):
        first = source * variables + v
        yield slice(0, whole), pl.ds(first, whole, stride=stride)
        for level in range(whole, levels):
            yield slice(level, level + 1), pl.ds(level * stride + first, 1)

    reaches = []
    while far_count > 1 and 2 ** len(reaches) < far_count // 2:
        reaches.append(2 ** len(reaches))

    def announce(turn):
        if turn < len(reaches):
            for way, distance in ((0, reaches[turn]), (1, -reaches[turn])):
                pl.semaphore_signal(
                    line_sem.at[turn, way], inc=1, device_id={"col": in_line(distance)}, device_id_type=MESH
                )

    def heard(turn):
        if 0 <= turn < len(reaches):
            for way in range(2):
                pl.semaphore_wait(line_sem.at[turn, way], 1)

    def build(step, first, last):
        points = points_ref[step]
        slot_ids = points // BCOLS
        within = points % BCOLS
        for source in range(blocks):
            lanes = slice(source * BCOLS, (source + 1) * BCOLS)
            block = me * blocks + source
            slots = slot_ids[:, lanes]
            offset = jnp.zeros_like(slots)
            for slot in range(SLOTS):
                rel = lists_ref[step, source, slot] - block + REACH
                rel = jnp.where(rel < 0, rel + all_blocks, rel)
                rel = jnp.where(rel >= all_blocks, rel - all_blocks, rel)
                offset = jnp.where(slots == slot, rel, offset)
            column = offset * BCOLS + within[:, lanes]
            weight = weights_ref[step][:, lanes]
            parity = source % 2
            pair = source // 2
            half = slice(parity * BCOLS, (parity + 1) * BCOLS)
            empty = jnp.zeros((BCOLS, BCOLS), BF16)
            unused = slice(0, BCOLS) if parity else slice(SLOTS * BCOLS, WINDOW)
            if first == 0:
                w_high[step, pair, unused, half] = empty
                w_low[step, pair, unused, half] = empty
            for piece in range(SLOTS):
                if not first <= source + piece <= last and not first <= blocks + 3 - source - piece <= last:
                    continue
                rows = lax.broadcasted_iota(jnp.int32, (BCOLS, BCOLS), 0) + piece * BCOLS
                total = jnp.zeros((BCOLS, BCOLS), F32)
                for point in range(POINTS):
                    hit = rows == column[point : point + 1]
                    total = total + jnp.where(hit, weight[point : point + 1], 0.0)
                high, low = halves(total)
                place = slice((piece + parity) * BCOLS, (piece + parity + 1) * BCOLS)
                w_high[step, pair, place, half] = high
                w_low[step, pair, place, half] = low

    def pad_inverse(step):
        for source in range(blocks):
            inv_pad[source] = jnp.zeros((padded, padded), F32)
            inv_pad[source, 0:levels, 0:levels] = inv_in[step, source]

    def stacked_inverse(source):
        high, low = halves(inv_pad[source])
        return jnp.concatenate([high, low, high], axis=0)

    def diffuse(inverse, value):
        high, low = halves(value)
        return lax.dot_general(
            inverse,
            jnp.concatenate([high, high, low], axis=0),
            (((0,), (0,)), ((), ())),
            preferred_element_type=F32,
        )

    def diffused_pairs(block_value, inverses, chosen=None):
        result = []
        for pair in range(pairs) if chosen is None else [chosen]:
            left = diffuse(inverses[2 * pair], block_value(2 * pair))
            right = diffuse(inverses[2 * pair + 1], block_value(2 * pair + 1))
            rows = [
                jnp.concatenate(
                    [left[:, v * BCOLS : (v + 1) * BCOLS], right[:, v * BCOLS : (v + 1) * BCOLS]], axis=1
                )
                for v in range(per_chunk)
            ]
            result.append(halves(jnp.concatenate(rows, axis=0)))
        return result

    def tile_sum(step, diffused, tile):
        left, right = [], []
        for pair in range(pairs):
            if 0 <= tile - pair <= 2:
                high, low = diffused[pair]
                place = slice((tile - pair) * PAIR, (tile - pair + 1) * PAIR)
                left += [high, low, high]
                matrix = w_high[step, pair, place, :]
                right += [matrix, matrix, w_low[step, pair, place, :]]
        return lax.dot_general(
            jnp.concatenate(left, axis=1),
            jnp.concatenate(right, axis=1),
            (((1,), (1,)), ((), ())),
            preferred_element_type=F32,
        )

    def halo_copy(exchange, chunk, way):
        return pltpu.make_async_remote_copy(
            src_ref=send_buf.at[exchange, chunk, way],
            dst_ref=recv_buf.at[exchange, chunk, way],
            send_sem=send_sem.at[exchange, chunk, way],
            recv_sem=recv_sem.at[exchange, chunk, way],
            device_id={"col": up if way else down},
            device_id_type=MESH,
        )

    def scatter(exchange, step, chunk, diffused, first, between):
        for way, tile in ((0, 0), (1, tiles - 1)):
            value = tile_sum(step, diffused, tile)
            for v in range(per_chunk):
                send_buf[exchange, chunk, way, v] = value[v * padded : v * padded + levels]
        if first:
            pl.semaphore_wait(barrier, len(adjacent))
        for way in range(2):
            halo_copy(exchange, chunk, way).start()
        between()
        for tile in range(1, tiles - 1):
            value = tile_sum(step, diffused, tile)
            for v in range(per_chunk):
                own[chunk * per_chunk + v, :, (tile - 1) * PAIR : tile * PAIR] = value[
                    v * padded : (v + 1) * padded
                ]

    def arrived_from(exchange, chunk, way):
        halo_copy(exchange, chunk, way).wait_recv()
        part = slice(0, levels)
        lanes = slice(0, PAIR) if way else slice(col_count - PAIR, col_count)
        for v in range(per_chunk):
            row = chunk * per_chunk + v
            own[row, part, lanes] = own[row, part, lanes] + recv_buf[exchange, chunk, way, v]

    def send_side(exchange, step, chunk, diffused, way):
        value = tile_sum(step, diffused, tiles - 1 if way else 0)
        for v in range(per_chunk):
            send_buf[exchange, chunk, way, v] = value[v * padded : v * padded + levels]
        halo_copy(exchange, chunk, way).start()

    def own_tiles(step, chunk, diffused):
        for tile in range(1, tiles - 1):
            value = tile_sum(step, diffused, tile)
            for v in range(per_chunk):
                own[chunk * per_chunk + v, :, (tile - 1) * PAIR : tile * PAIR] = value[
                    v * padded : (v + 1) * padded
                ]

    for copy in small_copies:
        copy.wait()
    build(1, 0, 1)
    for copy in inv_copies[1]:
        copy.wait()
    pad_inverse(1)
    inverses = [stacked_inverse(source) for source in range(blocks)]
    for v in range(variables):
        adj_pad[v, padded - 8 : padded, :] = jnp.zeros((8, col_count), F32)
    for chunk in range(CHUNKS):
        if chunk == 0:
            adj_copy.wait()
        for v in range(chunk * per_chunk, (chunk + 1) * per_chunk):
            for source in range(blocks):
                lanes = slice(source * BCOLS, (source + 1) * BCOLS)
                for part, rows in pieces(v, source):
                    adj_pad[v, part, lanes] = adj_in[rows, :]

        def block_value(source, chunk=chunk):
            lanes = slice(source * BCOLS, (source + 1) * BCOLS)
            return jnp.concatenate(
                [adj_pad[v, :, lanes] for v in range(chunk * per_chunk, (chunk + 1) * per_chunk)], axis=1
            )

        def rest_of_weights(chunk=chunk):
            if chunk == 0:
                announce(0)
                build(1, 2, 3)

        scatter(0, 1, chunk, diffused_pairs(block_value, inverses), chunk == 0, rest_of_weights)

    build(0, 0, 1)
    build(0, 2, 3)
    for copy in inv_copies[0]:
        copy.wait()
    pad_inverse(0)
    inverses = [stacked_inverse(source) for source in range(blocks)]
    heard(0)
    announce(1)
    for chunk in range(CHUNKS):
        def block_value(source, chunk=chunk):
            lanes = slice(source * BCOLS, (source + 1) * BCOLS)
            return jnp.concatenate(
                [own[v, :, lanes] for v in range(chunk * per_chunk, (chunk + 1) * per_chunk)], axis=1
            )

        def keep_mid(chunk=chunk):
            for v in range(chunk * per_chunk, (chunk + 1) * per_chunk):
                for source in range(blocks):
                    for part, rows in pieces(v, source):
                        mid_ref[rows, :] = own[v, part, source * BCOLS : (source + 1) * BCOLS]

        arrived_from(0, chunk, 1)
        low_side = diffused_pairs(block_value, inverses, 0)
        send_side(1, 0, chunk, low_side + [None], 0)
        arrived_from(0, chunk, 0)
        high_side = diffused_pairs(block_value, inverses, 1)
        send_side(1, 0, chunk, [None] + high_side, 1)
        keep_mid()
        own_tiles(0, chunk, low_side + high_side)
        if chunk == 1:
            heard(1)
            announce(2)

    total = jnp.zeros((8, BCOLS), F32)
    for chunk in range(CHUNKS):
        for way in (1, 0):
            arrived_from(1, chunk, way)
        for v in range(chunk * per_chunk, (chunk + 1) * per_chunk):
            value = own[v]
            square = value * value
            by_lane = square[:, 0:BCOLS]
            for block in range(1, blocks):
                by_lane = by_lane + square[:, block * BCOLS : (block + 1) * BCOLS]
            total = total + jnp.sum(by_lane.reshape(padded // 8, 8, BCOLS), axis=0)
    total = jnp.sum(total, axis=0, keepdims=True)

    near_buf[near_me] = total
    near_copies = [
        pltpu.make_async_remote_copy(
            src_ref=near_buf.at[near_me],
            dst_ref=near_buf.at[near_me],
            send_sem=near_send.at[j],
            recv_sem=near_recv.at[0],
            device_id={"col": peer},
            device_id_type=MESH,
        )
        for j, peer in enumerate(near_peers)
    ]
    for copy in near_copies:
        copy.start()
    for v in range(variables):
        for source in range(blocks):
            for part, rows in pieces(v, source):
                start_ref[rows, :] = own[v, part, source * BCOLS : (source + 1) * BCOLS]
    if group > 1:
        others = pl.ds(0, group - 1)
        pltpu.make_async_remote_copy(
            src_ref=near_buf.at[others],
            dst_ref=near_buf.at[others],
            send_sem=near_send.at[0],
            recv_sem=near_recv.at[0],
            device_id={"col": near_peers[0]},
            device_id_type=MESH,
        ).wait_recv()
    total = jnp.sum(near_buf[...], axis=0)
    far_buf[far_me] = total
    far_copies = [
        pltpu.make_async_remote_copy(
            src_ref=far_buf.at[far_me],
            dst_ref=far_buf.at[far_me],
            send_sem=far_send.at[j],
            recv_sem=far_recv.at[0],
            device_id={"col": peer},
            device_id_type=MESH,
        )
        for j, peer in enumerate(far_peers)
    ]
    for turn in range(2, len(reaches)):
        heard(turn)
        announce(turn + 1)
    for copy in far_copies:
        copy.start()
    if far_count > 1:
        others = pl.ds(0, far_count - 1)
        pltpu.make_async_remote_copy(
            src_ref=far_buf.at[others],
            dst_ref=far_buf.at[others],
            send_sem=far_send.at[0],
            recv_sem=far_recv.at[0],
            device_id={"col": far_peers[0]},
            device_id_type=MESH,
        ).wait_recv()
    total = jnp.sum(far_buf[...], axis=0)
    energy_ref[...] = total
    for exchange in range(2):
        for chunk in range(CHUNKS):
            for way in range(2):
                halo_copy(exchange, chunk, way).wait_send()
    for copy in near_copies + far_copies:
        copy.wait_send()


def finish(cells, mid_in, start_in, energy_ref, mid_hbm, out_hbm, scaled, sem):
    mid_copy = pltpu.make_async_copy(mid_in, mid_hbm, sem.at[0])
    mid_copy.start()
    energy = jnp.sum(energy_ref[...], axis=1, keepdims=True)
    scale = 1.0 / jnp.sqrt(energy / cells + EPS_ENERGY)
    size = scaled.shape[0] // FINISH_PARTS
    copies = [mid_copy]
    for piece in range(FINISH_PARTS):
        part = pl.ds(piece * size, size)
        scaled[part, :] = start_in[part, :] * scale
        copy = pltpu.make_async_copy(scaled.at[part], out_hbm.at[part], sem.at[1 + piece])
        copy.start()
        copies.append(copy)
    for copy in copies:
        copy.wait()


def shards(adj_final, inverses, dep_lists, dep_points, weights):
    variables, levels, col_count = adj_final.shape
    count = lax.axis_size("col")
    blocks = col_count // BCOLS
    padded = -(-levels // 16) * 16
    pairs = blocks // 2
    per_chunk = variables // CHUNKS
    group = min(GROUP, count)
    far_count = count // group
    halo = (2, CHUNKS, 2, per_chunk, levels, PAIR)
    rows = levels * blocks * variables
    like = jax.ShapeDtypeStruct((rows, BCOLS), F32)
    adj_rows = adj_final.reshape(variables, levels, blocks, BCOLS).transpose(1, 2, 0, 3).reshape(rows, BCOLS)
    vmem = pl.BlockSpec(memory_space=pltpu.VMEM)
    anywhere = pl.BlockSpec(memory_space=pltpu.HBM)
    mid, start, energy = pl.pallas_call(
        functools.partial(kernel, count),
        out_shape=(like, like, jax.ShapeDtypeStruct((1, BCOLS), F32)),
        in_specs=[pl.BlockSpec(memory_space=pltpu.HBM)] * 5,
        out_specs=(vmem, vmem, vmem),
        scratch_shapes=[
            pltpu.SMEM(dep_lists.shape, jnp.int32),
            pltpu.VMEM(dep_points.shape, jnp.int32),
            pltpu.VMEM(weights.shape, F32),
            pltpu.VMEM((rows, BCOLS), F32),
            pltpu.VMEM((STEPS, blocks, levels, levels), F32),
            pltpu.VMEM((variables, padded, col_count), F32),
            pltpu.VMEM((blocks, padded, padded), F32),
            pltpu.VMEM((STEPS, pairs, WINDOW, PAIR), BF16),
            pltpu.VMEM((STEPS, pairs, WINDOW, PAIR), BF16),
            pltpu.VMEM((variables, padded, col_count), F32),
            pltpu.VMEM(halo, F32),
            pltpu.VMEM(halo, F32),
            pltpu.VMEM((group, 1, BCOLS), F32),
            pltpu.VMEM((far_count, 1, BCOLS), F32),
            pltpu.SemaphoreType.REGULAR((8, 2)),
            pltpu.SemaphoreType.DMA((3,)),
            pltpu.SemaphoreType.DMA((1,)),
            pltpu.SemaphoreType.DMA((STEPS, blocks)),
            pltpu.SemaphoreType.DMA((2, CHUNKS, 2)),
            pltpu.SemaphoreType.DMA((2, CHUNKS, 2)),
            pltpu.SemaphoreType.DMA((group,)),
            pltpu.SemaphoreType.DMA((group,)),
            pltpu.SemaphoreType.DMA((far_count,)),
            pltpu.SemaphoreType.DMA((far_count,)),
        ],
        compiler_params=pltpu.CompilerParams(
            collective_id=0, has_side_effects=True, vmem_limit_bytes=48 << 20
        ),
    )(
        *(
            pltpu.with_memory_space_constraint(value, pltpu.HBM)
            for value in (dep_lists, dep_points, weights, adj_rows, inverses.transpose(0, 2, 1, 3))
        )
    )
    outs = pl.pallas_call(
        functools.partial(finish, count * adj_final.size),
        out_shape=(like, like),
        in_specs=[vmem, vmem, vmem],
        out_specs=(anywhere, anywhere),
        scratch_shapes=[pltpu.VMEM((rows, BCOLS), F32), pltpu.SemaphoreType.DMA((1 + FINISH_PARTS,))],
        compiler_params=pltpu.CompilerParams(vmem_limit_bytes=16 << 20),
    )(mid, start, energy)
    return tuple(
        out.reshape(levels, blocks, variables, BCOLS).transpose(2, 0, 1, 3).reshape(adj_final.shape)
        for out in outs
    )


def solution(mesh):
    in_specs = (
        P("mem", None, "col"),
        P("mem", "col", None, None),
        P("mem", "col", None),
        P("mem", None, "col"),
        P("mem", None, "col"),
    )
    out_specs = (P("mem", None, "col"), P("mem", None, "col"))
    return jax.shard_map(shards, mesh=mesh, in_specs=in_specs, out_specs=out_specs, check_vma=False)
```
